32 devices in a mesh: seq: 2 (over x), tok: 16 (over z, y, core).
Axes of the slice: x: 2, y: 2, z: 4, core: 2. Of those that a mesh axis runs over, the one named last changes fastest.
Arguments:
- queries: bfloat16 [8192, 4096], P(('seq', 'tok')), parts along dimension 0, may hold values from -6 to 6
- keys: bfloat16 [8192, 4096], P(('seq', 'tok')), parts along dimension 0, may hold values from -6 to 6
- values: bfloat16 [8192, 4096], P(('seq', 'tok')), parts along dimension 0, may hold values from -6 to 6
- segments: int32 [8192], P(('seq', 'tok')), parts along dimension 0, may hold values from 0 to 31, never falling along the last dimension, each value on 1 to 256 neighbouring positions
- short_filters: bfloat16 [3, 3, 4096], replicated, may hold values from -3.5 to 3.5
- mr_filter: bfloat16 [128, 256], replicated, may hold values from -0.5 to 0.5
- mr_bias: bfloat16 [4096], replicated, may hold values from -1 to 1
Outputs:
- mixed: bfloat16 [8192, 4096], P(('seq', 'tok')), parts along dimension 0
The draws below stay inside these ranges and needn't reach their ends.
There are 2 independent parts, one for each index of `seq`. The reference program is written for one: setup_inputs(seed, part) draws one part's arguments, and reference() takes and returns one part's arrays. A program takes and returns all parts, laid end to end along the dimension named above; an argument that names none is the same for every part. Nothing has to cross between parts.
Inputs may be any that keep to these rules, and one draw needn't show every extreme that they name: `segments`: document numbers never fall along the window; each document spans 1 to 256 positions, and one spans exactly 256.
All inputs are finite; a program needn't handle non-finite values.
Results may differ from the reference program's by a relative error of at most 0.0049.
Values may be sent and summed in bfloat16 or wider, within the bound.
A program may use at most 128 MiB of HBM per device.

```python
import math
import jax
import jax.numpy as jnp
import numpy as np
from jax import lax

D = 4096
GROUPS = 256
SHORT = 3
LONG = 128
TOK_DEV = 256
LENGTH = 4096
N_TOK = 16


def levels(own_key, dims, split, least, high):
    gain = 1.0
    for axis_at, blocks in split:
        draws = jax.random.uniform(jax.random.fold_in(jax.random.fold_in(own_key, 6), axis_at), (blocks,), jnp.float32, least / len(split), high / len(split))
        gain = gain * jnp.repeat(jnp.exp(draws), dims[axis_at] // blocks).reshape((-1,) + (1,) * (len(dims) - 1 - axis_at))
    return gain


def profile(amount, total, reach, skew):
    loads = [(1 << 20) // math.isqrt(grade ** skew) + 1 for grade in range(2, amount + 1)]
    rest, counts = total - reach - (amount - 1), [1] * (amount - 1)
    while rest > 0:
        candidates = [i for i in range(amount - 1) if counts[i] < reach]
        pool, left = sum([loads[i] for i in candidates]), rest
        for i in candidates:
            more = min(reach - counts[i], max(1, left * loads[i] // pool), rest)
            counts[i] = counts[i] + more
            rest = rest - more
    return np.array([reach] + counts)


def ragged_sizes(stream_key, number_of, total, reach, lean):
    if number_of == 2:
        one = jax.random.randint(stream_key, (), max(1, total - reach), min(reach, total - 1) + 1)
        return jnp.stack([one, total - one])
    sizes = jnp.asarray(profile(number_of, total, reach, lean), jnp.int32)
    twos = (number_of - 1) // 2
    donor, taker = sizes[1:1 + 2 * twos:2], sizes[2:2 + 2 * twos:2]
    slack = jnp.minimum(donor - 1, reach - taker)
    shifted = jax.random.randint(jax.random.fold_in(stream_key, 1), (twos,), 0, 1 << 20) % (slack + 1)
    sizes = sizes.at[1:1 + 2 * twos:2].set(donor - shifted).at[2:2 + 2 * twos:2].set(taker + shifted)
    return sizes[jax.random.permutation(jax.random.fold_in(stream_key, 2), number_of)]


def scatter_about(own_key, shape, spread, limit, pieces=(), kind=jnp.bfloat16):
    entries = spread * jax.random.normal(own_key, shape, jnp.float32)
    if pieces:
        entries = entries * levels(own_key, shape, pieces, -0.22, 0.18)
    return jnp.clip(entries, -limit, limit).astype(kind)


def setup_inputs(seed: int = 0, part: int = 0) -> dict:
    arg_keys = jax.random.split(jax.random.key(seed), 8)
    part_splits = jax.random.split(jax.random.fold_in(arg_keys[7], part), 8)
    return {
        "queries": scatter_about(part_splits[0], (LENGTH, D), 1.0, 6.0, ((0, 16),)),
        "keys": scatter_about(part_splits[1], (LENGTH, D), 1.0, 6.0, ((0, 16),)),
        "values": scatter_about(part_splits[2], (LENGTH, D), 1.0, 6.0, ((0, 16),)),
        "segments": jnp.searchsorted(jnp.cumsum(ragged_sizes(part_splits[3], 2 * N_TOK, LENGTH, TOK_DEV, 2)), jnp.arange(LENGTH), side="right").astype(jnp.int32),
        "short_filters": scatter_about(arg_keys[4], (3, SHORT, D), SHORT ** -0.5, 3.5),
        "mr_filter": scatter_about(arg_keys[5], (LONG, GROUPS), LONG ** -0.5, 0.5),
        "mr_bias": jnp.clip(jax.random.uniform(arg_keys[6], (D,), jnp.float32, -1.0, 1.0), -1.0, 1.0).astype(jnp.bfloat16),
    }


def short_mix(extended, marks, taps, count):
    width = taps.shape[0]
    anchor = marks[width - 1:width - 1 + count]
    total = jnp.zeros((count, extended.shape[1]), jnp.float32)
    for offset in range(width):
        begin = width - 1 - offset
        same = (marks[begin:begin + count] == anchor).astype(jnp.float32)
        total = total + taps[offset].astype(jnp.float32)[None, :] * extended[begin:begin + count].astype(jnp.float32) * same[:, None]
    return total


def long_mix(extended, marks, filters, bias, count):
    block = filters.shape[0]
    groups = filters.shape[1]
    width = extended.shape[1]
    members = width // groups
    blocks = count // block
    earlier = extended[:count].reshape(blocks, block, width)
    current = extended[block:].reshape(blocks, block, width)
    windows = jnp.concatenate([earlier, current], 1).reshape(blocks, 2 * block, groups, members)
    mark_cols = jnp.concatenate([marks[:count].reshape(blocks, block), marks[block:].reshape(blocks, block)], 1)
    mark_rows = marks[block:].reshape(blocks, block)
    row_index = jnp.arange(block)[:, None]
    col_index = jnp.arange(2 * block)[None, :]
    offset = row_index + block - col_index
    valid = (offset >= 0) & (offset < block)
    table = filters.astype(jnp.float32)[jnp.clip(offset, 0, block - 1)]
    table = jnp.where(valid[:, :, None], table, jnp.zeros((), jnp.float32))
    table = jnp.transpose(table, (2, 0, 1))

    def one_block(items):
        window, mark_col, mark_row = items
        same = (mark_col[None, :] == mark_row[:, None]).astype(jnp.float32)
        matrix = table * same[None]
        result = jnp.einsum('gij,jgc->igc', matrix, window.astype(jnp.float32))
        return result.reshape(block, width)

    result = lax.map(one_block, (windows, mark_cols, mark_rows)).reshape(count, width)
    return result + bias.astype(jnp.float32)[None, :] * extended[block:].astype(jnp.float32)


def reference(queries, keys, values, segments, short_filters, mr_filter, mr_bias):
    count = queries.shape[0]
    width = queries.shape[1]
    front = jnp.zeros((SHORT - 1, width), jnp.bfloat16)
    marks_short = jnp.concatenate([jnp.full((SHORT - 1,), -1, jnp.int32), segments.astype(jnp.int32)])
    feat_q = short_mix(jnp.concatenate([front, queries]), marks_short, short_filters[0], count)
    feat_k = short_mix(jnp.concatenate([front, keys]), marks_short, short_filters[1], count)
    feat_v = short_mix(jnp.concatenate([front, values]), marks_short, short_filters[2], count)
    product = (feat_k * feat_v).astype(jnp.bfloat16)
    extended = jnp.concatenate([jnp.zeros((LONG, width), jnp.bfloat16), product])
    marks_long = jnp.concatenate([jnp.full((LONG,), -1, jnp.int32), segments.astype(jnp.int32)])
    longer = long_mix(extended, marks_long, mr_filter, mr_bias, count)
    return (feat_q * longer).astype(jnp.bfloat16)
```

```python
import functools

import jax
import jax.numpy as jnp
from jax import lax
from jax.experimental import pallas as pl
from jax.experimental.pallas import tpu as pltpu
from jax.sharding import PartitionSpec as P

LANES = 128
TILE = 512
CHUNKS = 4


def shifted(value, axis, by):
    size = lax.axis_size(axis)
    pairs = [(i, i + by) for i in range(size) if 0 <= i + by < size]
    return lax.ppermute(value, axis, pairs)


def column(row, block):
    return jnp.transpose(jnp.broadcast_to(row, (block, block)))


def feature(x, before, taps, one, two):
    x = x.astype(jnp.float32)
    before = before.astype(jnp.float32)
    taps = taps.astype(jnp.float32)
    at = lax.broadcasted_iota(jnp.int32, x.shape, 0)
    far, near = before[0:1], before[1:2]
    x1 = jnp.where(at == 0, near, pltpu.roll(x, 1, 0))
    x2 = jnp.where(at == 0, far, jnp.where(at == 1, near, pltpu.roll(x, 2, 0)))
    return taps[0:1] * x + (taps[1:2] * x1) * one + (taps[2:3] * x2) * two


def short_marks(info, start, block):
    return (
        column(info[1:2, start : start + block], block),
        column(info[2:3, start : start + block], block),
    )


def tail_kernel(k, v, ke, ve, taps, info, out, one_ref, two_ref):
    block = k.shape[0]

    @pl.when(pl.program_id(0) == 0)
    def _():
        one_ref[...], two_ref[...] = short_marks(info, 2 * block, block)

    one, two = one_ref[...], two_ref[...]
    for s in range(0, k.shape[1], LANES):
        at = slice(s, s + LANES)
        fk = feature(k[:, at], ke[14:16, at], taps[1, :, at], one, two)
        fv = feature(v[:, at], ve[14:16, at], taps[2, :, at], one, two)
        out[:, at] = (fk * fv).astype(out.dtype)


def prepare(info, filters, hrev, upper, lower, start, block):
    tap = lax.broadcasted_iota(jnp.int32, (block, block), 0)
    lane = lax.broadcasted_iota(jnp.int32, (block, block), 1)
    turn = (tap == lax.rem(block - lane, block)).astype(jnp.bfloat16)
    hrev[...] = lax.dot_general(
        filters[...], turn, (((0,), (0,)), ((), ())), preferred_element_type=jnp.float32
    )
    own = column(info[0:1, start : start + block], block)
    prev_row = info[0:1, start - block : start]
    own_row = info[0:1, start : start + block]
    upper[...] = jnp.where((own == prev_row) & (lane > tap), 1.0, 0.0).astype(jnp.bfloat16)
    lower[...] = jnp.where((own == own_row) & (lane <= tap), 1.0, 0.0).astype(jnp.bfloat16)


def long_tile(prev, cur, hrev, first, members, upper, lower):
    block = prev.shape[0]
    window = jnp.concatenate([prev, cur], 0)
    lane = lax.broadcasted_iota(jnp.int32, (block, LANES), 1)
    total = None
    for g in range(LANES // members):
        base = jnp.broadcast_to(hrev[pl.ds(first + g, 1), :], (block, block))
        ring = pltpu.roll(base, 0, 1, stride=1, stride_axis=0).astype(jnp.bfloat16)
        table = jnp.concatenate([ring * upper, ring * lower], 1)
        part = jnp.dot(table, window, preferred_element_type=jnp.float32)
        total = part if g == 0 else jnp.where(lane < g * members, total, part)
    return total


def back_kernel(members, q, qe, k, v, edge, ptail, taps, bias, info, filters,
                out, phead, hrev, upper, lower, one_ref, two_ref, hone_ref, htwo_ref):
    block = q.shape[0]
    step = pl.program_id(0)

    @pl.when(step == 0)
    def _():
        prepare(info, filters, hrev, upper, lower, 2 * block, block)
        one_ref[...], two_ref[...] = short_marks(info, 2 * block, block)
        hone_ref[...], htwo_ref[...] = short_marks(info, block, block)

    up, low = upper[...], lower[...]
    per = LANES // members
    for s in range(0, q.shape[1], LANES):
        at = slice(s, s + LANES)
        hone, htwo = hone_ref[...], htwo_ref[...]
        fk = feature(k[:, at], edge[2:4, at], taps[1, :, at], hone, htwo)
        fv = feature(v[:, at], edge[4:6, at], taps[2, :, at], hone, htwo)
        prev = (fk * fv).astype(jnp.bfloat16)
        phead[:, at] = prev
        cur = ptail[:, at]
        first = step * (q.shape[1] // members) + (s // LANES) * per
        longer = long_tile(prev, cur, hrev, first, members, up, low)
        longer = longer + bias[:, at].astype(jnp.float32) * cur.astype(jnp.float32)
        fq = feature(q[:, at], qe[14:16, at], taps[0, :, at], one_ref[...], two_ref[...])
        out[:, at] = (fq * longer).astype(out.dtype)


def front_kernel(members, base, q, edge, halo, phead, taps, bias, info, filters, whole,
                 out, hrev, upper, lower, one_ref, two_ref):
    del whole
    block = q.shape[0]
    step = pl.program_id(0)

    @pl.when(step == 0)
    def _():
        prepare(info, filters, hrev, upper, lower, block, block)
        one_ref[...], two_ref[...] = short_marks(info, block, block)

    up, low = upper[...], lower[...]
    per = LANES // members
    for s in range(0, q.shape[1], LANES):
        at = slice(s, s + LANES)
        cur = phead[:, at]
        first = (base + step) * (q.shape[1] // members) + (s // LANES) * per
        longer = long_tile(halo[:, at], cur, hrev, first, members, up, low)
        longer = longer + bias[:, at].astype(jnp.float32) * cur.astype(jnp.float32)
        fq = feature(q[:, at], edge[0:2, at], taps[0, :, at], one_ref[...], two_ref[...])
        out[:, at] = (fq * longer).astype(out.dtype)


def marks_of(segments_ext):
    seg = segments_ext.astype(jnp.float32)
    one = jnp.concatenate([jnp.zeros((1,), jnp.float32), (seg[1:] == seg[:-1]).astype(jnp.float32)])
    two = jnp.concatenate([jnp.zeros((2,), jnp.float32), (seg[2:] == seg[:-2]).astype(jnp.float32)])
    return jnp.stack([seg, one, two])


def per_device(queries, keys, values, segments, short_filters, mr_filter, mr_bias):
    rows, width = queries.shape
    block, groups = mr_filter.shape
    members = width // groups
    reach = short_filters.shape[1]
    tile = min(TILE, width // CHUNKS)
    sub = block // 16
    bf16, f32 = jnp.bfloat16, jnp.float32
    bias = mr_bias.reshape(1, width)
    edge = jnp.concatenate([x[rows - (reach - 1):] for x in (queries, keys, values)])
    edge = shifted(edge, "tok", 1)
    edge_marks = shifted(segments[rows - block:], "tok", 1)
    info_own = marks_of(jnp.concatenate([jnp.zeros((block,), jnp.int32), segments]))
    info = marks_of(jnp.concatenate([edge_marks, segments]))

    full = lambda a: pl.BlockSpec(a.shape, lambda c: (0,) * a.ndim)
    blk = lambda r: pl.BlockSpec((block, tile), lambda c: (r, c))
    last = pl.BlockSpec((16, tile), lambda c: (sub - 1, c))
    tap_spec = pl.BlockSpec((3, reach, tile), lambda c: (0, 0, c))
    square = lambda t: pltpu.VMEM((block, block), t)
    row = pl.BlockSpec((1, tile), lambda c: (0, c))
    edge_spec = pl.BlockSpec((edge.shape[0], tile), lambda c: (0, c))
    half_shape = jax.ShapeDtypeStruct((block, width), bf16)

    ptail = pl.pallas_call(
        tail_kernel,
        grid=(width // tile,),
        in_specs=[blk(1), blk(1), last, last, tap_spec, full(info_own)],
        out_specs=blk(0),
        out_shape=half_shape,
        scratch_shapes=[square(f32), square(f32)],
        cost_estimate=pl.CostEstimate(flops=10**7, bytes_accessed=3 * 2**20, transcendentals=0),
    )(keys, values, keys, values, short_filters, info_own)

    cut = width // CHUNKS
    halos = [shifted(ptail[:, i * cut : (i + 1) * cut], "tok", 1) for i in range(CHUNKS)]

    out, phead = pl.pallas_call(
        functools.partial(back_kernel, members),
        grid=(width // tile,),
        in_specs=[blk(1), last, blk(0), blk(0), edge_spec, blk(0), tap_spec, row,
                  full(info), full(mr_filter)],
        out_specs=[blk(1), blk(0)],
        out_shape=[jax.ShapeDtypeStruct((rows, width), bf16), half_shape],
        scratch_shapes=[pltpu.VMEM((groups, block), f32), square(bf16), square(bf16)]
        + [square(f32)] * 4,
        cost_estimate=pl.CostEstimate(flops=10**10, bytes_accessed=6 * 2**20, transcendentals=0),
    )(queries, queries, keys, values, edge, ptail, short_filters, bias, info, mr_filter)

    for i in range(CHUNKS):
        base = i * (cut // tile)
        off = lambda shape, z, base=base: pl.BlockSpec(shape, lambda c: z + (base + c,))
        out = pl.pallas_call(
            functools.partial(front_kernel, members, base),
            grid=(cut // tile,),
            in_specs=[
                off((block, tile), (0,)),
                off((edge.shape[0], tile), (0,)),
                pl.BlockSpec((block, tile), lambda c: (0, c)),
                off((block, tile), (0,)),
                off((3, reach, tile), (0, 0)),
                off((1, tile), (0,)),
                full(info),
                full(mr_filter),
                pl.BlockSpec(memory_space=pl.ANY),
            ],
            out_specs=off((block, tile), (0,)),
            out_shape=jax.ShapeDtypeStruct((rows, width), bf16),
            input_output_aliases={8: 0},
            scratch_shapes=[pltpu.VMEM((groups, block), f32), square(bf16), square(bf16)]
            + [square(f32)] * 2,
            cost_estimate=pl.CostEstimate(
                flops=10**10 // CHUNKS, bytes_accessed=4 * 2**20 // CHUNKS, transcendentals=0
            ),
        )(queries, edge, halos[i], phead, short_filters, bias, info, mr_filter, out)
    return out


def solution(mesh):
    placed = (
        P(("seq", "tok"), None),
        P(("seq", "tok"), None),
        P(("seq", "tok"), None),
        P(("seq", "tok")),
        P(),
        P(),
        P(),
    )
    return jax.shard_map(
        per_device, mesh=mesh, in_specs=placed, out_specs=P(("seq", "tok"), None), check_vma=False
    )
```

```python
import functools

import jax
import jax.numpy as jnp
from jax import lax
from jax.experimental import pallas as pl
from jax.experimental.pallas import tpu as pltpu
from jax.sharding import PartitionSpec as P

LANES = 128
TILE = 512
F32, BF16 = jnp.float32, jnp.bfloat16


def column(row, block):
    return jnp.transpose(jnp.broadcast_to(row, (block, block)))


def feature(x, before, taps, one, two):
    x = x.astype(F32)
    at = lax.broadcasted_iota(jnp.int32, x.shape, 0)
    far, near = before[0:1], before[1:2]
    x1 = jnp.where(at == 0, near, pltpu.roll(x, 1, 0))
    x2 = jnp.where(at == 0, far, jnp.where(at == 1, near, pltpu.roll(x, 2, 0)))
    return taps[0:1] * x + (taps[1:2] * x1) * one + (taps[2:3] * x2) * two


def kernel(axis, members, tiles, q, k, v, seg_hbm, taps_hbm, filters_hbm, bias_hbm, out,
           seg, taps, filters, bias, qb, kb, vb, pt, halo, raw, edge_send, edge, seg_prev, hrev, biasf,
           table0, table1, masks, shorts,
           small_sem, raw_sem, tail_sem, head_sem, q_sem,
           send_sem, recv_sem, small_send, small_recv):
    rows, width = q.shape
    block = filters.shape[0]
    tile = width // tiles
    per = LANES // members
    keep = block - 16
    me = lax.axis_index(axis)
    size = lax.axis_size(axis)
    has_left, has_right = me > 0, me < size - 1
    left, right = jnp.maximum(me - 1, 0), jnp.minimum(me + 1, size - 1)
    barrier = pltpu.get_barrier_semaphore()

    @pl.when(has_left)
    def _():
        pl.semaphore_signal(barrier, inc=1, device_id={axis: left}, device_id_type=pl.DeviceIdType.MESH)

    @pl.when(has_right)
    def _():
        pl.semaphore_signal(barrier, inc=1, device_id={axis: right}, device_id_type=pl.DeviceIdType.MESH)

    def cols(c):
        return pl.ds(pl.multiple_of(c * tile, tile), tile)

    def raw_copy(i):
        return pltpu.make_async_copy((q, k, v)[i].at[pl.ds(rows - 8, 8)], raw.at[i], raw_sem.at[i])

    def tail_copy(i, c):
        at = pl.ds(keep, rows - keep)
        return pltpu.make_async_copy(
            (k, v)[i].at[at, cols(c)], (kb, vb)[i].at[c, at], tail_sem.at[i, c])

    def head_copy(i, c):
        at = pl.ds(0, keep)
        return pltpu.make_async_copy(
            (k, v)[i].at[at, cols(c)], (kb, vb)[i].at[c, at], head_sem.at[i, c])

    def q_copy(c):
        return pltpu.make_async_copy(q.at[:, cols(c)], qb.at[c], q_sem.at[c])

    def remote(src, dst, s, r):
        return pltpu.make_async_remote_copy(
            src_ref=src, dst_ref=dst, send_sem=s, recv_sem=r,
            device_id={axis: right}, device_id_type=pl.DeviceIdType.MESH)

    def product_copy(c):
        return remote(pt.at[c], halo.at[c], send_sem.at[c], recv_sem.at[c])

    def edge_copy():
        return remote(edge_send, edge, small_send.at[0], small_recv.at[0])

    def seg_copy():
        return remote(seg, seg_prev, small_send.at[1], small_recv.at[1])

    small = [
        pltpu.make_async_copy(src, dst, small_sem.at[i])
        for i, (src, dst) in enumerate(
            ((seg_hbm, seg), (taps_hbm, taps), (filters_hbm, filters), (bias_hbm, bias)))
    ]
    small[0].start()
    for i in range(3):
        raw_copy(i).start()
    small[1].start()

    @pl.loop(0, tiles)
    def _(c):
        tail_copy(0, c).start()
        tail_copy(1, c).start()

    small[2].start()
    small[3].start()

    @pl.loop(0, tiles)
    def _(c):
        head_copy(0, c).start()
        head_copy(1, c).start()
        q_copy(c).start()

    tap = lax.broadcasted_iota(jnp.int32, (block, block), 0)
    lane = lax.broadcasted_iota(jnp.int32, (block, block), 1)

    def make_masks(b, row_before, row):
        own, early = column(row, block), column(row_before, block)
        one = jnp.where(tap == 0, pltpu.roll(early, 1, 0), pltpu.roll(own, 1, 0))
        two = jnp.where(tap < 2, pltpu.roll(early, 2, 0), pltpu.roll(own, 2, 0))
        shorts[b, 0] = jnp.where(own == one, 1.0, 0.0)
        shorts[b, 1] = jnp.where(own == two, 1.0, 0.0)
        masks[b, 0] = jnp.where((own == row_before) & (lane > tap), 1.0, 0.0).astype(BF16)
        masks[b, 1] = jnp.where((own == row) & (lane <= tap), 1.0, 0.0).astype(BF16)

    small[0].wait()
    seg0, seg1 = seg[0:1].astype(F32), seg[1:2].astype(F32)
    make_masks(1, seg0, seg1)
    for i in range(3):
        raw_copy(i).wait()
    edge_send[...] = jnp.concatenate(
        [raw[i].astype(F32)[6:8] for i in range(3)] + [jnp.zeros((2, width), F32)]).astype(BF16)
    for copy in small[1:]:
        copy.wait()
    turn = (tap == lax.rem(block - lane, block)).astype(BF16)
    hrev[...] = lax.dot_general(
        filters[...], turn, (((0,), (0,)), ((), ())), preferred_element_type=F32)
    biasf[...] = bias[...].astype(F32)
    pl.semaphore_wait(barrier, has_left.astype(jnp.int32) + has_right.astype(jnp.int32))

    @pl.when(has_right)
    def _():
        seg_copy().start()
        edge_copy().start()

    def part(c, s):
        return pl.ds(pl.multiple_of(c * tile + s, LANES), LANES)

    def taps_of(i, at):
        return taps[i, :, at].astype(F32)

    @pl.loop(0, tiles)
    def _(c):
        tail_copy(0, c).wait()
        tail_copy(1, c).wait()
        for s in range(0, tile, LANES):
            at, here = part(c, s), slice(s, s + LANES)
            one, two = shorts[1, 0], shorts[1, 1]
            feats = []
            for i, buf in ((1, kb), (2, vb)):
                before = buf[c, keep:block, here].astype(F32)[14:16]
                feats.append(feature(buf[c, block:, here], before, taps_of(i, at), one, two))
            pt[c, :, here] = (feats[0] * feats[1]).astype(BF16)

        @pl.when(has_right & (c > 0))
        def _():
            product_copy(jnp.maximum(c - 1, 0)).start()

    @pl.when(has_right)
    def _():
        product_copy(tiles - 1).start()

    @pl.when(has_left)
    def _():
        seg_copy().wait_recv()
        edge_copy().wait_recv()

    @pl.when(jnp.logical_not(has_left))
    def _():
        seg_prev[...] = jnp.zeros_like(seg_prev)
        edge[...] = jnp.zeros_like(edge)

        @pl.loop(0, tiles)
        def _(c):
            halo[c] = jnp.zeros_like(halo[c])

    make_masks(0, seg_prev[1:2].astype(F32), seg0)
    glane = lane // members

    @pl.loop(0, tiles)
    def _(c):
        head_copy(0, c).wait()
        head_copy(1, c).wait()
        q_copy(c).wait()

        @pl.when(has_left)
        def _():
            product_copy(c).wait_recv()

        for s in range(0, tile, LANES):
            at, here = part(c, s), slice(s, s + LANES)
            edges = edge[:, at].astype(F32)
            one, two = shorts[0, 0], shorts[0, 1]
            fk = feature(kb[c, :block, here], edges[2:4], taps_of(1, at), one, two)
            fv = feature(vb[c, :block, here], edges[4:6], taps_of(2, at), one, two)
            mid = (fk * fv).astype(BF16)
            far, near = halo[c, :, here], pt[c, :, here]
            first = (c * tile + s) // members
            for g in range(per):
                base = jnp.broadcast_to(hrev[pl.ds(first + g, 1), :], (block, block))
                ring = pltpu.roll(base, 0, 1, stride=1, stride_axis=0).astype(BF16)
                here_rows = slice(g * block, (g + 1) * block)
                table0[here_rows, :block] = ring * masks[0, 0]
                table0[here_rows, block:] = ring * masks[0, 1]
                table1[here_rows, :block] = ring * masks[1, 0]
                table1[here_rows, block:] = ring * masks[1, 1]
            brow = biasf[pl.ds((c * tile + s) // LANES, 1), :]
            for b, (table, low, high) in enumerate(((table0, far, mid), (table1, mid, near))):
                every = jnp.dot(table[...], jnp.concatenate([low, high], 0),
                                preferred_element_type=F32)
                longer = every[:block]
                for g in range(1, per):
                    longer = jnp.where(glane < g, longer, every[g * block : (g + 1) * block])
                longer = longer + brow * high.astype(F32)
                if b == 0:
                    before = edges[0:2]
                else:
                    before = qb[c, keep:block, here].astype(F32)[14:16]
                own = slice(b * block, (b + 1) * block)
                fq = feature(qb[c, own, here], before, taps_of(0, at), shorts[b, 0], shorts[b, 1])
                out[own, at] = (fq * longer).astype(BF16)

    @pl.when(has_right)
    def _():
        seg_copy().wait_send()
        edge_copy().wait_send()

        @pl.loop(0, tiles)
        def _(c):
            product_copy(c).wait_send()


def per_device(queries, keys, values, segments, short_filters, mr_filter, mr_bias):
    rows, width = queries.shape
    block, groups = mr_filter.shape
    members = width // groups
    tile = min(TILE, width)
    tiles = width // tile
    per = LANES // members
    dma = pltpu.SemaphoreType.DMA
    chunked = lambda r: pltpu.VMEM((tiles, r, tile), BF16)
    return pl.pallas_call(
        functools.partial(kernel, "tok", members, tiles),
        in_specs=[pl.BlockSpec(memory_space=pltpu.HBM)] * 7,
        out_specs=pl.BlockSpec(memory_space=pltpu.VMEM),
        out_shape=jax.ShapeDtypeStruct((rows, width), BF16),
        scratch_shapes=[
            pltpu.VMEM((rows // block, block), jnp.int32),
            pltpu.VMEM(short_filters.shape, BF16),
            pltpu.VMEM(mr_filter.shape, BF16),
            pltpu.VMEM((width // LANES, LANES), BF16),
            chunked(rows), chunked(rows), chunked(rows),
            chunked(block), chunked(block),
            pltpu.VMEM((3, 8, width), BF16),
            pltpu.VMEM((8, width), BF16),
            pltpu.VMEM((8, width), BF16),
            pltpu.VMEM((rows // block, block), jnp.int32),
            pltpu.VMEM((groups, block), F32),
            pltpu.VMEM((width // LANES, LANES), F32),
            pltpu.VMEM((per * block, 2 * block), BF16),
            pltpu.VMEM((per * block, 2 * block), BF16),
            pltpu.VMEM((2, 2, block, block), BF16),
            pltpu.VMEM((2, 2, block, block), F32),
            dma((4,)), dma((3,)), dma((2, tiles)), dma((2, tiles)), dma((tiles,)),
            dma((tiles,)), dma((tiles,)), dma((2,)), dma((2,)),
        ],
        compiler_params=pltpu.CompilerParams(collective_id=0, has_side_effects=True),
    )(queries, keys, values, segments.reshape(rows // block, block), short_filters,
      mr_filter, mr_bias.reshape(width // LANES, LANES))


def solution(mesh):
    placed = (
        P(("seq", "tok"), None),
        P(("seq", "tok"), None),
        P(("seq", "tok"), None),
        P(("seq", "tok")),
        P(),
        P(),
        P(),
    )
    return jax.shard_map(
        per_device, mesh=mesh, in_specs=placed, out_specs=P(("seq", "tok"), None), check_vma=False
    )
```

```python
import functools

import jax
import jax.numpy as jnp
from jax import lax
from jax.experimental import pallas as pl
from jax.experimental.pallas import tpu as pltpu
from jax.sharding import PartitionSpec as P

LANES = 128
TILE = 512
F32, BF16 = jnp.float32, jnp.bfloat16


def column(row, block):
    return jnp.transpose(jnp.broadcast_to(row, (block, block)))


def feature(x, before, taps, one, two):
    x = x.astype(F32)
    at = lax.broadcasted_iota(jnp.int32, x.shape, 0)
    far, near = before[0:1], before[1:2]
    x1 = jnp.where(at == 0, near, pltpu.roll(x, 1, 0))
    x2 = jnp.where(at == 0, far, jnp.where(at == 1, near, pltpu.roll(x, 2, 0)))
    return taps[0:1] * x + (taps[1:2] * x1) * one + (taps[2:3] * x2) * two


def kernel(axis, members, tiles, q, k, v, seg_hbm, taps_hbm, filters_hbm, bias_hbm, out,
           seg, taps, filters, bias, qb, kb, vb, pt, halo, raw, edge_send, edge, seg_prev, hrev, biasf,
           table0, table1, masks, shorts,
           small_sem, raw_sem, tail_sem, head_sem, q_sem,
           send_sem, recv_sem, small_send, small_recv):
    rows, width = q.shape
    block = filters.shape[0]
    tile = width // tiles
    per = LANES // members
    keep = block - 16
    me = lax.axis_index(axis)
    size = lax.axis_size(axis)
    has_left, has_right = me > 0, me < size - 1
    left, right = jnp.maximum(me - 1, 0), jnp.minimum(me + 1, size - 1)
    barrier = pltpu.get_barrier_semaphore()

    @pl.when(has_left)
    def _():
        pl.semaphore_signal(barrier, inc=1, device_id={axis: left}, device_id_type=pl.DeviceIdType.MESH)

    @pl.when(has_right)
    def _():
        pl.semaphore_signal(barrier, inc=1, device_id={axis: right}, device_id_type=pl.DeviceIdType.MESH)

    def cols(c):
        return pl.ds(pl.multiple_of(c * tile, tile), tile)

    def raw_copy(i):
        return pltpu.make_async_copy((q, k, v)[i].at[pl.ds(rows - 8, 8)], raw.at[i], raw_sem.at[i])

    def tail_copy(i, c):
        at = pl.ds(keep, rows - keep)
        return pltpu.make_async_copy(
            (k, v)[i].at[at, cols(c)], (kb, vb)[i].at[c, at], tail_sem.at[i, c])

    def head_copy(i, c):
        at = pl.ds(0, keep)
        return pltpu.make_async_copy(
            (k, v)[i].at[at, cols(c)], (kb, vb)[i].at[c, at], head_sem.at[i, c])

    def q_copy(c):
        return pltpu.make_async_copy(q.at[:, cols(c)], qb.at[c], q_sem.at[c])

    def remote(src, dst, s, r):
        return pltpu.make_async_remote_copy(
            src_ref=src, dst_ref=dst, send_sem=s, recv_sem=r,
            device_id={axis: right}, device_id_type=pl.DeviceIdType.MESH)

    def product_copy(c):
        return remote(pt.at[c], halo.at[c], send_sem.at[c], recv_sem.at[c])

    def edge_copy():
        return remote(edge_send, edge, small_send.at[0], small_recv.at[0])

    def seg_copy():
        return remote(seg, seg_prev, small_send.at[1], small_recv.at[1])

    small = [
        pltpu.make_async_copy(src, dst, small_sem.at[i])
        for i, (src, dst) in enumerate(
            ((seg_hbm, seg), (taps_hbm, taps), (filters_hbm, filters), (bias_hbm, bias)))
    ]
    small[0].start()
    for i in range(3):
        raw_copy(i).start()
    small[1].start()

    @pl.loop(0, tiles)
    def _(c):
        tail_copy(0, c).start()
        tail_copy(1, c).start()

    small[2].start()
    small[3].start()

    @pl.loop(0, tiles)
    def _(c):
        head_copy(0, c).start()
        head_copy(1, c).start()
        q_copy(c).start()

    tap = lax.broadcasted_iota(jnp.int32, (block, block), 0)
    lane = lax.broadcasted_iota(jnp.int32, (block, block), 1)

    def make_masks(b, row_before, row):
        own, early = column(row, block), column(row_before, block)
        one = jnp.where(tap == 0, pltpu.roll(early, 1, 0), pltpu.roll(own, 1, 0))
        two = jnp.where(tap < 2, pltpu.roll(early, 2, 0), pltpu.roll(own, 2, 0))
        shorts[b, 0] = jnp.where(own == one, 1.0, 0.0)
        shorts[b, 1] = jnp.where(own == two, 1.0, 0.0)
        masks[b, 0] = jnp.where((own == row_before) & (lane > tap), 1.0, 0.0).astype(BF16)
        masks[b, 1] = jnp.where((own == row) & (lane <= tap), 1.0, 0.0).astype(BF16)

    small[0].wait()
    seg0, seg1 = seg[0:1].astype(F32), seg[1:2].astype(F32)
    make_masks(1, seg0, seg1)
    for i in range(3):
        raw_copy(i).wait()
    edge_send[...] = jnp.concatenate(
        [raw[i].astype(F32)[6:8] for i in range(3)] + [jnp.zeros((2, width), F32)]).astype(BF16)
    for copy in small[1:]:
        copy.wait()
    turn = (tap == lax.rem(block - lane, block)).astype(BF16)
    hrev[...] = lax.dot_general(
        filters[...], turn, (((0,), (0,)), ((), ())), preferred_element_type=F32)
    biasf[...] = bias[...].astype(F32)
    pl.semaphore_wait(barrier, has_left.astype(jnp.int32) + has_right.astype(jnp.int32))

    @pl.when(has_right)
    def _():
        seg_copy().start()
        edge_copy().start()

    def part(c, s):
        return pl.ds(pl.multiple_of(c * tile + s, LANES), LANES)

    def taps_of(i, at):
        return taps[i, :, at].astype(F32)

    @pl.loop(0, tiles)
    def _(c):
        tail_copy(0, c).wait()
        tail_copy(1, c).wait()
        for s in range(0, tile, LANES):
            at, here = part(c, s), slice(s, s + LANES)
            one, two = shorts[1, 0], shorts[1, 1]
            feats = []
            for i, buf in ((1, kb), (2, vb)):
                before = buf[c, keep:block, here].astype(F32)[14:16]
                feats.append(feature(buf[c, block:, here], before, taps_of(i, at), one, two))
            pt[c, :, here] = (feats[0] * feats[1]).astype(BF16)

        @pl.when(has_right & (c > 0))
        def _():
            product_copy(jnp.maximum(c - 1, 0)).start()

    @pl.when(has_right)
    def _():
        product_copy(tiles - 1).start()

    @pl.when(has_left)
    def _():
        seg_copy().wait_recv()
        edge_copy().wait_recv()

    @pl.when(jnp.logical_not(has_left))
    def _():
        seg_prev[...] = jnp.zeros_like(seg_prev)
        edge[...] = jnp.zeros_like(edge)

        @pl.loop(0, tiles)
        def _(c):
            halo[c] = jnp.zeros_like(halo[c])

    make_masks(0, seg_prev[1:2].astype(F32), seg0)
    glane = lane // members

    @pl.loop(0, tiles)
    def _(c):
        head_copy(0, c).wait()
        head_copy(1, c).wait()
        q_copy(c).wait()

        @pl.when(has_left)
        def _():
            product_copy(c).wait_recv()

        for s in range(0, tile, LANES):
            at, here = part(c, s), slice(s, s + LANES)
            edges = edge[:, at].astype(F32)
            one, two = shorts[0, 0], shorts[0, 1]
            fk = feature(kb[c, :block, here], edges[2:4], taps_of(1, at), one, two)
            fv = feature(vb[c, :block, here], edges[4:6], taps_of(2, at), one, two)
            mid = (fk * fv).astype(BF16)
            far, near = halo[c, :, here], pt[c, :, here]
            first = (c * tile + s) // members
            for g in range(per):
                base = jnp.broadcast_to(hrev[pl.ds(first + g, 1), :], (block, block))
                ring = pltpu.roll(base, 0, 1, stride=1, stride_axis=0).astype(BF16)
                here_rows = slice(g * block, (g + 1) * block)
                table0[here_rows, :block] = ring * masks[0, 0]
                table0[here_rows, block:] = ring * masks[0, 1]
                table1[here_rows, :block] = ring * masks[1, 0]
                table1[here_rows, block:] = ring * masks[1, 1]
            brow = biasf[pl.ds((c * tile + s) // LANES, 1), :]
            for b, (table, low, high) in enumerate(((table0, far, mid), (table1, mid, near))):
                every = jnp.dot(table[...], jnp.concatenate([low, high], 0),
                                preferred_element_type=F32)
                longer = every[:block]
                for g in range(1, per):
                    longer = jnp.where(glane < g, longer, every[g * block : (g + 1) * block])
                longer = longer + brow * high.astype(F32)
                if b == 0:
                    before = edges[0:2]
                else:
                    before = qb[c, keep:block, here].astype(F32)[14:16]
                own = slice(b * block, (b + 1) * block)
                fq = feature(qb[c, own, here], before, taps_of(0, at), shorts[b, 0], shorts[b, 1])
                out[own, at] = (fq * longer).astype(BF16)

    @pl.when(has_right)
    def _():
        seg_copy().wait_send()
        edge_copy().wait_send()

        @pl.loop(0, tiles)
        def _(c):
            product_copy(c).wait_send()


def per_device(queries, keys, values, segments, short_filters, mr_filter, mr_bias):
    rows, width = queries.shape
    block, groups = mr_filter.shape
    members = width // groups
    tile = min(TILE, width)
    tiles = width // tile
    per = LANES // members
    dma = pltpu.SemaphoreType.DMA
    chunked = lambda r: pltpu.VMEM((tiles, r, tile), BF16)
    return pl.pallas_call(
        functools.partial(kernel, "tok", members, tiles),
        in_specs=[pl.BlockSpec(memory_space=pltpu.HBM)] * 7,
        out_specs=pl.BlockSpec(memory_space=pltpu.VMEM),
        out_shape=pltpu.VMEM((rows, width), BF16),
        scratch_shapes=[
            pltpu.VMEM((rows // block, block), jnp.int32),
            pltpu.VMEM(short_filters.shape, BF16),
            pltpu.VMEM(mr_filter.shape, BF16),
            pltpu.VMEM((width // LANES, LANES), BF16),
            chunked(rows), chunked(rows), chunked(rows),
            chunked(block), chunked(block),
            pltpu.VMEM((3, 8, width), BF16),
            pltpu.VMEM((8, width), BF16),
            pltpu.VMEM((8, width), BF16),
            pltpu.VMEM((rows // block, block), jnp.int32),
            pltpu.VMEM((groups, block), F32),
            pltpu.VMEM((width // LANES, LANES), F32),
            pltpu.VMEM((per * block, 2 * block), BF16),
            pltpu.VMEM((per * block, 2 * block), BF16),
            pltpu.VMEM((2, 2, block, block), BF16),
            pltpu.VMEM((2, 2, block, block), F32),
            dma((4,)), dma((3,)), dma((2, tiles)), dma((2, tiles)), dma((tiles,)),
            dma((tiles,)), dma((tiles,)), dma((2,)), dma((2,)),
        ],
        compiler_params=pltpu.CompilerParams(
            collective_id=0, has_side_effects=True, vmem_limit_bytes=28 * 2**20
        ),
    )(*(pltpu.with_memory_space_constraint(x, pltpu.HBM) for x in (
        queries, keys, values, segments.reshape(rows // block, block), short_filters,
        mr_filter, mr_bias.reshape(width // LANES, LANES))))


def solution(mesh):
    placed = (
        P(("seq", "tok"), None),
        P(("seq", "tok"), None),
        P(("seq", "tok"), None),
        P(("seq", "tok")),
        P(),
        P(),
        P(),
    )
    return jax.shard_map(
        per_device, mesh=mesh, in_specs=placed, out_specs=P(("seq", "tok"), None), check_vma=False
    )
```

```python
import functools

import jax
import jax.numpy as jnp
from jax import lax
from jax.experimental import pallas as pl
from jax.experimental.pallas import tpu as pltpu
from jax.sharding import PartitionSpec as P

LANES = 128
TILE = 512
F32, BF16 = jnp.float32, jnp.bfloat16


def column(row, block):
    return jnp.transpose(jnp.broadcast_to(row, (block, block)))


def feature(x, before, taps, one, two):
    x = x.astype(F32)
    at = lax.broadcasted_iota(jnp.int32, x.shape, 0)
    far, near = before[0:1], before[1:2]
    x1 = jnp.where(at == 0, near, pltpu.roll(x, 1, 0))
    x2 = jnp.where(at == 0, far, jnp.where(at == 1, near, pltpu.roll(x, 2, 0)))
    return taps[0:1] * x + (taps[1:2] * x1) * one + (taps[2:3] * x2) * two


def kernel(axis, members, tiles, q, k, v, seg_hbm, taps_hbm, filters_hbm, bias_hbm, out,
           seg, taps, filters, bias, qb, kb, vb, pt, halo, raw, edge_send, edge, seg_prev, hrev, biasf,
           table0, table1, picked, masks, shorts,
           small_sem, raw_sem, tail_sem, head_sem, q_sem,
           send_sem, recv_sem, small_send, small_recv):
    rows, width = q.shape
    block = filters.shape[0]
    tile = width // tiles
    per = LANES // members
    keep = block - 16
    me = lax.axis_index(axis)
    size = lax.axis_size(axis)
    has_left, has_right = me > 0, me < size - 1
    left, right = jnp.maximum(me - 1, 0), jnp.minimum(me + 1, size - 1)
    barrier = pltpu.get_barrier_semaphore()

    @pl.when(has_left)
    def _():
        pl.semaphore_signal(barrier, inc=1, device_id={axis: left}, device_id_type=pl.DeviceIdType.MESH)

    @pl.when(has_right)
    def _():
        pl.semaphore_signal(barrier, inc=1, device_id={axis: right}, device_id_type=pl.DeviceIdType.MESH)

    def cols(c):
        return pl.ds(pl.multiple_of(c * tile, tile), tile)

    def raw_copy(i):
        return pltpu.make_async_copy((q, k, v)[i].at[pl.ds(rows - 8, 8)], raw.at[i], raw_sem.at[i])

    def tail_copy(i, c):
        at = pl.ds(keep, rows - keep)
        return pltpu.make_async_copy(
            (k, v)[i].at[at, cols(c)], (kb, vb)[i].at[c, at], tail_sem.at[i, c])

    def head_copy(i, c):
        at = pl.ds(0, keep)
        return pltpu.make_async_copy(
            (k, v)[i].at[at, cols(c)], (kb, vb)[i].at[c, at], head_sem.at[i, c])

    def q_copy(c):
        return pltpu.make_async_copy(q.at[:, cols(c)], qb.at[c], q_sem.at[c])

    def remote(src, dst, s, r):
        return pltpu.make_async_remote_copy(
            src_ref=src, dst_ref=dst, send_sem=s, recv_sem=r,
            device_id={axis: right}, device_id_type=pl.DeviceIdType.MESH)

    def product_copy(c):
        return remote(pt.at[c], halo.at[c], send_sem.at[c], recv_sem.at[c])

    def edge_copy():
        return remote(edge_send, edge, small_send.at[0], small_recv.at[0])

    def seg_copy():
        return remote(seg, seg_prev, small_send.at[1], small_recv.at[1])

    small = [
        pltpu.make_async_copy(src, dst, small_sem.at[i])
        for i, (src, dst) in enumerate(
            ((seg_hbm, seg), (taps_hbm, taps), (filters_hbm, filters), (bias_hbm, bias)))
    ]
    small[0].start()
    for i in range(3):
        raw_copy(i).start()
    small[1].start()

    @pl.loop(0, tiles)
    def _(c):
        tail_copy(0, c).start()
        tail_copy(1, c).start()

    small[2].start()
    small[3].start()

    @pl.loop(0, tiles)
    def _(c):
        head_copy(0, c).start()
        head_copy(1, c).start()
        q_copy(c).start()

    tap = lax.broadcasted_iota(jnp.int32, (block, block), 0)
    lane = lax.broadcasted_iota(jnp.int32, (block, block), 1)

    def make_masks(b, row_before, row):
        own, early = column(row, block), column(row_before, block)
        one = jnp.where(tap == 0, pltpu.roll(early, 1, 0), pltpu.roll(own, 1, 0))
        two = jnp.where(tap < 2, pltpu.roll(early, 2, 0), pltpu.roll(own, 2, 0))
        shorts[b, 0] = jnp.where(own == one, 1.0, 0.0)
        shorts[b, 1] = jnp.where(own == two, 1.0, 0.0)
        masks[b, 0] = jnp.where((own == row_before) & (lane > tap), 1.0, 0.0).astype(BF16)
        masks[b, 1] = jnp.where((own == row) & (lane <= tap), 1.0, 0.0).astype(BF16)

    small[0].wait()
    seg0, seg1 = seg[0:1].astype(F32), seg[1:2].astype(F32)
    make_masks(1, seg0, seg1)
    for i in range(3):
        raw_copy(i).wait()
    edge_send[...] = jnp.concatenate(
        [raw[i].astype(F32)[6:8] for i in range(3)] + [jnp.zeros((2, width), F32)]).astype(BF16)
    pl.semaphore_wait(barrier, has_left.astype(jnp.int32) + has_right.astype(jnp.int32))

    @pl.when(has_right)
    def _():
        seg_copy().start()
        edge_copy().start()

    def part(c, s):
        return pl.ds(pl.multiple_of(c * tile + s, LANES), LANES)

    def taps_of(i, at):
        return taps[i, :, at].astype(F32)

    small[1].wait()

    @pl.loop(0, tiles)
    def _(c):
        tail_copy(0, c).wait()
        tail_copy(1, c).wait()
        for s in range(0, tile, LANES):
            at, here = part(c, s), slice(s, s + LANES)
            one, two = shorts[1, 0], shorts[1, 1]
            feats = []
            for i, buf in ((1, kb), (2, vb)):
                before = buf[c, keep:block, here].astype(F32)[14:16]
                feats.append(feature(buf[c, block:, here], before, taps_of(i, at), one, two))
            pt[c, :, here] = (feats[0] * feats[1]).astype(BF16)

        @pl.when(has_right & (c > 0))
        def _():
            product_copy(jnp.maximum(c - 1, 0)).start()

    @pl.when(has_right)
    def _():
        product_copy(tiles - 1).start()

    small[2].wait()
    small[3].wait()
    turn = (tap == lax.rem(block - lane, block)).astype(BF16)
    hrev[...] = lax.dot_general(
        filters[...], turn, (((0,), (0,)), ((), ())), preferred_element_type=F32)
    biasf[...] = bias[...].astype(F32)

    @pl.when(has_left)
    def _():
        seg_copy().wait_recv()
        edge_copy().wait_recv()

    @pl.when(jnp.logical_not(has_left))
    def _():
        seg_prev[...] = jnp.zeros_like(seg_prev)
        edge[...] = jnp.zeros_like(edge)

        @pl.loop(0, tiles)
        def _(c):
            halo[c] = jnp.zeros_like(halo[c])

    make_masks(0, seg_prev[1:2].astype(F32), seg0)
    glane = lane // members

    @pl.loop(0, tiles)
    def _(c):
        head_copy(0, c).wait()
        head_copy(1, c).wait()
        q_copy(c).wait()

        @pl.when(has_left)
        def _():
            product_copy(c).wait_recv()

        for s in range(0, tile, LANES):
            at, here = part(c, s), slice(s, s + LANES)
            edges = edge[:, at].astype(F32)
            one, two = shorts[0, 0], shorts[0, 1]
            fk = feature(kb[c, :block, here], edges[2:4], taps_of(1, at), one, two)
            fv = feature(vb[c, :block, here], edges[4:6], taps_of(2, at), one, two)
            mid = (fk * fv).astype(BF16)
            far, near = halo[c, :, here], pt[c, :, here]
            first = (c * tile + s) // members
            for g in range(per):
                base = jnp.broadcast_to(hrev[pl.ds(first + g, 1), :], (block, block))
                ring = pltpu.roll(base, 0, 1, stride=1, stride_axis=0).astype(BF16)
                here_rows = slice(g * block, (g + 1) * block)
                table0[here_rows, :block] = ring * masks[0, 0]
                table0[here_rows, block:] = ring * masks[0, 1]
                table1[here_rows, :block] = ring * masks[1, 0]
                table1[here_rows, block:] = ring * masks[1, 1]
            brow = biasf[pl.ds((c * tile + s) // LANES, 1), :]
            for b, (table, low, high) in enumerate(((table0, far, mid), (table1, mid, near))):
                every = jnp.dot(table[...], jnp.concatenate([low, high], 0),
                                preferred_element_type=F32)
                for g in range(per):
                    pltpu.store(picked.at[b], every[g * block : (g + 1) * block], mask=glane == g)
                longer = picked[b] + brow * high.astype(F32)
                if b == 0:
                    before = edges[0:2]
                else:
                    before = qb[c, keep:block, here].astype(F32)[14:16]
                own = slice(b * block, (b + 1) * block)
                fq = feature(qb[c, own, here], before, taps_of(0, at), shorts[b, 0], shorts[b, 1])
                out[own, at] = (fq * longer).astype(BF16)

    @pl.when(has_right)
    def _():
        seg_copy().wait_send()
        edge_copy().wait_send()

        @pl.loop(0, tiles)
        def _(c):
            product_copy(c).wait_send()


def per_device(queries, keys, values, segments, short_filters, mr_filter, mr_bias):
    rows, width = queries.shape
    block, groups = mr_filter.shape
    members = width // groups
    tile = min(TILE, width)
    tiles = width // tile
    per = LANES // members
    dma = pltpu.SemaphoreType.DMA
    chunked = lambda r: pltpu.VMEM((tiles, r, tile), BF16)
    return pl.pallas_call(
        functools.partial(kernel, "tok", members, tiles),
        in_specs=[pl.BlockSpec(memory_space=pltpu.HBM)] * 7,
        out_specs=pl.BlockSpec(memory_space=pltpu.VMEM),
        out_shape=pltpu.VMEM((rows, width), BF16),
        scratch_shapes=[
            pltpu.VMEM((rows // block, block), jnp.int32),
            pltpu.VMEM(short_filters.shape, BF16),
            pltpu.VMEM(mr_filter.shape, BF16),
            pltpu.VMEM((width // LANES, LANES), BF16),
            chunked(rows), chunked(rows), chunked(rows),
            chunked(block), chunked(block),
            pltpu.VMEM((3, 8, width), BF16),
            pltpu.VMEM((8, width), BF16),
            pltpu.VMEM((8, width), BF16),
            pltpu.VMEM((rows // block, block), jnp.int32),
            pltpu.VMEM((groups, block), F32),
            pltpu.VMEM((width // LANES, LANES), F32),
            pltpu.VMEM((per * block, 2 * block), BF16),
            pltpu.VMEM((per * block, 2 * block), BF16),
            pltpu.VMEM((2, block, LANES), F32),
            pltpu.VMEM((2, 2, block, block), BF16),
            pltpu.VMEM((2, 2, block, block), F32),
            dma((4,)), dma((3,)), dma((2, tiles)), dma((2, tiles)), dma((tiles,)),
            dma((tiles,)), dma((tiles,)), dma((2,)), dma((2,)),
        ],
        compiler_params=pltpu.CompilerParams(
            collective_id=0, has_side_effects=True, vmem_limit_bytes=28 * 2**20
        ),
    )(*(pltpu.with_memory_space_constraint(x, pltpu.HBM) for x in (
        queries, keys, values, segments.reshape(rows // block, block), short_filters,
        mr_filter, mr_bias.reshape(width // LANES, LANES))))


def solution(mesh):
    placed = (
        P(("seq", "tok"), None),
        P(("seq", "tok"), None),
        P(("seq", "tok"), None),
        P(("seq", "tok")),
        P(),
        P(),
        P(),
    )
    return jax.shard_map(
        per_device, mesh=mesh, in_specs=placed, out_specs=P(("seq", "tok"), None), check_vma=False
    )
```

```python
import functools

import jax
import jax.numpy as jnp
from jax import lax
from jax.experimental import pallas as pl
from jax.experimental.pallas import tpu as pltpu
from jax.sharding import PartitionSpec as P

LANES = 128
TILE = 512
F32, BF16 = jnp.float32, jnp.bfloat16


def column(row, block):
    return jnp.transpose(jnp.broadcast_to(row, (block, block)))


def feature(x, before, taps, one, two):
    x = x.astype(F32)
    at = lax.broadcasted_iota(jnp.int32, x.shape, 0)
    far, near = before[0:1], before[1:2]
    x1 = jnp.where(at == 0, near, pltpu.roll(x, 1, 0))
    x2 = jnp.where(at == 0, far, jnp.where(at == 1, near, pltpu.roll(x, 2, 0)))
    return taps[0:1] * x + (taps[1:2] * x1) * one + (taps[2:3] * x2) * two


def kernel(axis, members, tiles, q, k, v, seg_hbm, taps_hbm, filters_hbm, bias_hbm, out,
           seg, taps, filters, bias, qb, kb, vb, pt, halo, raw, edge_send, edge, seg_prev, hrev, biasf,
           table0, table1, picked, masks, shorts,
           small_sem, raw_sem, tail_sem, head_sem, q_sem,
           send_sem, recv_sem, small_send, small_recv):
    rows, width = q.shape
    block = filters.shape[0]
    tile = width // tiles
    per = LANES // members
    keep = block - 16
    me = lax.axis_index(axis)
    size = lax.axis_size(axis)
    has_left, has_right = me > 0, me < size - 1
    left, right = jnp.maximum(me - 1, 0), jnp.minimum(me + 1, size - 1)
    barrier = pltpu.get_barrier_semaphore()

    @pl.when(has_left)
    def _():
        pl.semaphore_signal(barrier, inc=1, device_id={axis: left}, device_id_type=pl.DeviceIdType.MESH)

    @pl.when(has_right)
    def _():
        pl.semaphore_signal(barrier, inc=1, device_id={axis: right}, device_id_type=pl.DeviceIdType.MESH)

    def cols(c):
        return pl.ds(pl.multiple_of(c * tile, tile), tile)

    def raw_copy(i):
        return pltpu.make_async_copy((q, k, v)[i].at[pl.ds(rows - 8, 8)], raw.at[i], raw_sem.at[i])

    def tail_copy(i, c):
        at = pl.ds(keep, rows - keep)
        return pltpu.make_async_copy(
            (k, v)[i].at[at, cols(c)], (kb, vb)[i].at[c, at], tail_sem.at[i, c])

    def head_copy(i, c):
        at = pl.ds(0, keep)
        return pltpu.make_async_copy(
            (k, v)[i].at[at, cols(c)], (kb, vb)[i].at[c, at], head_sem.at[i, c])

    def q_copy(c):
        return pltpu.make_async_copy(q.at[:, cols(c)], qb.at[c], q_sem.at[c])

    def remote(src, dst, s, r):
        return pltpu.make_async_remote_copy(
            src_ref=src, dst_ref=dst, send_sem=s, recv_sem=r,
            device_id={axis: right}, device_id_type=pl.DeviceIdType.MESH)

    def product_copy(c):
        return remote(pt.at[c], halo.at[c], send_sem.at[c], recv_sem.at[c])

    def edge_copy():
        return remote(edge_send, edge, small_send.at[0], small_recv.at[0])

    def seg_copy():
        return remote(seg, seg_prev, small_send.at[1], small_recv.at[1])

    small = [
        pltpu.make_async_copy(src, dst, small_sem.at[i])
        for i, (src, dst) in enumerate(
            ((seg_hbm, seg), (taps_hbm, taps), (filters_hbm, filters), (bias_hbm, bias)))
    ]
    small[0].start()
    for i in range(3):
        raw_copy(i).start()
    small[1].start()

    @pl.loop(0, tiles)
    def _(c):
        tail_copy(0, c).start()
        tail_copy(1, c).start()

    small[2].start()
    small[3].start()

    @pl.loop(0, tiles)
    def _(c):
        head_copy(0, c).start()
        head_copy(1, c).start()
        q_copy(c).start()

    tap = lax.broadcasted_iota(jnp.int32, (block, block), 0)
    lane = lax.broadcasted_iota(jnp.int32, (block, block), 1)

    def make_masks(b, row_before, row):
        own, early = column(row, block), column(row_before, block)
        one = jnp.where(tap == 0, pltpu.roll(early, 1, 0), pltpu.roll(own, 1, 0))
        two = jnp.where(tap < 2, pltpu.roll(early, 2, 0), pltpu.roll(own, 2, 0))
        shorts[b, 0] = jnp.where(own == one, 1.0, 0.0)
        shorts[b, 1] = jnp.where(own == two, 1.0, 0.0)
        masks[b, 0] = jnp.where((own == row_before) & (lane > tap), 1.0, 0.0).astype(BF16)
        masks[b, 1] = jnp.where((own == row) & (lane <= tap), 1.0, 0.0).astype(BF16)

    small[0].wait()
    seg0, seg1 = seg[0:1].astype(F32), seg[1:2].astype(F32)
    for i in range(3):
        raw_copy(i).wait()
    edge_send[...] = jnp.concatenate(
        [raw[i].astype(F32)[6:8] for i in range(3)] + [jnp.zeros((2, width), F32)]).astype(BF16)
    pl.semaphore_wait(barrier, has_left.astype(jnp.int32) + has_right.astype(jnp.int32))

    @pl.when(has_right)
    def _():
        seg_copy().start()
        edge_copy().start()

    make_masks(1, seg0, seg1)

    def part(c, s):
        return pl.ds(pl.multiple_of(c * tile + s, LANES), LANES)

    def taps_of(i, at):
        return taps[i, :, at].astype(F32)

    small[1].wait()

    @pl.loop(0, tiles)
    def _(c):
        tail_copy(0, c).wait()
        tail_copy(1, c).wait()
        for s in range(0, tile, LANES):
            at, here = part(c, s), slice(s, s + LANES)
            one, two = shorts[1, 0], shorts[1, 1]
            feats = []
            for i, buf in ((1, kb), (2, vb)):
                before = buf[c, keep:block, here].astype(F32)[14:16]
                feats.append(feature(buf[c, block:, here], before, taps_of(i, at), one, two))
            pt[c, :, here] = (feats[0] * feats[1]).astype(BF16)

        @pl.when(has_right & (c > 0))
        def _():
            product_copy(jnp.maximum(c - 1, 0)).start()

    @pl.when(has_right)
    def _():
        product_copy(tiles - 1).start()

    small[2].wait()
    small[3].wait()
    turn = (tap == lax.rem(block - lane, block)).astype(BF16)
    hrev[...] = lax.dot_general(
        filters[...], turn, (((0,), (0,)), ((), ())), preferred_element_type=F32)
    biasf[...] = bias[...].astype(F32)

    @pl.when(has_left)
    def _():
        seg_copy().wait_recv()
        edge_copy().wait_recv()

    @pl.when(jnp.logical_not(has_left))
    def _():
        seg_prev[...] = jnp.zeros_like(seg_prev)
        edge[...] = jnp.zeros_like(edge)

        @pl.loop(0, tiles)
        def _(c):
            halo[c] = jnp.zeros_like(halo[c])

    make_masks(0, seg_prev[1:2].astype(F32), seg0)
    glane = lane // members

    @pl.loop(0, tiles)
    def _(c):
        head_copy(0, c).wait()
        head_copy(1, c).wait()
        q_copy(c).wait()

        @pl.when(has_left)
        def _():
            product_copy(c).wait_recv()

        for s in range(0, tile, LANES):
            at, here = part(c, s), slice(s, s + LANES)
            edges = edge[:, at].astype(F32)
            one, two = shorts[0, 0], shorts[0, 1]
            fk = feature(kb[c, :block, here], edges[2:4], taps_of(1, at), one, two)
            fv = feature(vb[c, :block, here], edges[4:6], taps_of(2, at), one, two)
            mid = (fk * fv).astype(BF16)
            far, near = halo[c, :, here], pt[c, :, here]
            first = (c * tile + s) // members
            for g in range(per):
                base = jnp.broadcast_to(hrev[pl.ds(first + g, 1), :], (block, block))
                ring = pltpu.roll(base, 0, 1, stride=1, stride_axis=0).astype(BF16)
                here_rows = slice(g * block, (g + 1) * block)
                table0[here_rows, :block] = ring * masks[0, 0]
                table0[here_rows, block:] = ring * masks[0, 1]
                table1[here_rows, :block] = ring * masks[1, 0]
                table1[here_rows, block:] = ring * masks[1, 1]
            brow = biasf[pl.ds((c * tile + s) // LANES, 1), :]
            for b, (table, low, high) in enumerate(((table0, far, mid), (table1, mid, near))):
                every = jnp.dot(table[...], jnp.concatenate([low, high], 0),
                                preferred_element_type=F32)
                for g in range(per):
                    pltpu.store(picked.at[b], every[g * block : (g + 1) * block], mask=glane == g)
                longer = picked[b] + brow * high.astype(F32)
                if b == 0:
                    before = edges[0:2]
                else:
                    before = qb[c, keep:block, here].astype(F32)[14:16]
                own = slice(b * block, (b + 1) * block)
                fq = feature(qb[c, own, here], before, taps_of(0, at), shorts[b, 0], shorts[b, 1])
                out[own, at] = (fq * longer).astype(BF16)

    @pl.when(has_right)
    def _():
        seg_copy().wait_send()
        edge_copy().wait_send()

        @pl.loop(0, tiles)
        def _(c):
            product_copy(c).wait_send()


def per_device(queries, keys, values, segments, short_filters, mr_filter, mr_bias):
    rows, width = queries.shape
    block, groups = mr_filter.shape
    members = width // groups
    tile = min(TILE, width)
    tiles = width // tile
    per = LANES // members
    dma = pltpu.SemaphoreType.DMA
    chunked = lambda r: pltpu.VMEM((tiles, r, tile), BF16)
    return pl.pallas_call(
        functools.partial(kernel, "tok", members, tiles),
        in_specs=[pl.BlockSpec(memory_space=pltpu.HBM)] * 7,
        out_specs=pl.BlockSpec(memory_space=pltpu.VMEM),
        out_shape=pltpu.VMEM((rows, width), BF16),
        scratch_shapes=[
            pltpu.VMEM((rows // block, block), jnp.int32),
            pltpu.VMEM(short_filters.shape, BF16),
            pltpu.VMEM(mr_filter.shape, BF16),
            pltpu.VMEM((width // LANES, LANES), BF16),
            chunked(rows), chunked(rows), chunked(rows),
            chunked(block), chunked(block),
            pltpu.VMEM((3, 8, width), BF16),
            pltpu.VMEM((8, width), BF16),
            pltpu.VMEM((8, width), BF16),
            pltpu.VMEM((rows // block, block), jnp.int32),
            pltpu.VMEM((groups, block), F32),
            pltpu.VMEM((width // LANES, LANES), F32),
            pltpu.VMEM((per * block, 2 * block), BF16),
            pltpu.VMEM((per * block, 2 * block), BF16),
            pltpu.VMEM((2, block, LANES), F32),
            pltpu.VMEM((2, 2, block, block), BF16),
            pltpu.VMEM((2, 2, block, block), F32),
            dma((4,)), dma((3,)), dma((2, tiles)), dma((2, tiles)), dma((tiles,)),
            dma((tiles,)), dma((tiles,)), dma((2,)), dma((2,)),
        ],
        compiler_params=pltpu.CompilerParams(
            collective_id=0, has_side_effects=True, vmem_limit_bytes=28 * 2**20
        ),
    )(*(pltpu.with_memory_space_constraint(x, pltpu.HBM) for x in (
        queries, keys, values, segments.reshape(rows // block, block), short_filters,
        mr_filter, mr_bias.reshape(width // LANES, LANES))))


def solution(mesh):
    placed = (
        P(("seq", "tok"), None),
        P(("seq", "tok"), None),
        P(("seq", "tok"), None),
        P(("seq", "tok")),
        P(),
        P(),
        P(),
    )
    return jax.shard_map(
        per_device, mesh=mesh, in_specs=placed, out_specs=P(("seq", "tok"), None), check_vma=False
    )
```

```python
import functools

import jax
import jax.numpy as jnp
from jax import lax
from jax.experimental import pallas as pl
from jax.experimental.pallas import tpu as pltpu
from jax.sharding import PartitionSpec as P

LANES = 128
TILE = 512
F32, BF16 = jnp.float32, jnp.bfloat16


def column(row, block):
    return jnp.transpose(jnp.broadcast_to(row, (block, block)))


def feature(x, before, taps, one, two):
    x = x.astype(F32)
    at = lax.broadcasted_iota(jnp.int32, x.shape, 0)
    far, near = before[0:1], before[1:2]
    x1 = jnp.where(at == 0, near, pltpu.roll(x, 1, 0))
    x2 = jnp.where(at == 0, far, jnp.where(at == 1, near, pltpu.roll(x, 2, 0)))
    return taps[0:1] * x + (taps[1:2] * x1) * one + (taps[2:3] * x2) * two


def kernel(axis, members, tiles, q, k, v, seg_hbm, taps_hbm, filters_hbm, bias_hbm, out,
           seg, taps, filters, bias, qb, kb, vb, pt, halo, raw, edge_send, edge, seg_prev, hrev, biasf,
           table0, table1, picked, masks, shorts,
           small_sem, raw_sem, tail_sem, head_sem, q_sem,
           send_sem, recv_sem, small_send, small_recv):
    rows, width = q.shape
    block = filters.shape[0]
    tile = width // tiles
    per = LANES // members
    keep = block - 16
    me = lax.axis_index(axis)
    size = lax.axis_size(axis)
    has_left, has_right = me > 0, me < size - 1
    left, right = jnp.maximum(me - 1, 0), jnp.minimum(me + 1, size - 1)
    barrier = pltpu.get_barrier_semaphore()

    @pl.when(has_left)
    def _():
        pl.semaphore_signal(barrier, inc=1, device_id={axis: left}, device_id_type=pl.DeviceIdType.MESH)

    @pl.when(has_right)
    def _():
        pl.semaphore_signal(barrier, inc=1, device_id={axis: right}, device_id_type=pl.DeviceIdType.MESH)

    def cols(c):
        return pl.ds(pl.multiple_of(c * tile, tile), tile)

    def raw_copy(i):
        return pltpu.make_async_copy((q, k, v)[i].at[pl.ds(rows - 8, 8)], raw.at[i], raw_sem.at[i])

    def tail_copy(i, c):
        at = pl.ds(keep, rows - keep)
        return pltpu.make_async_copy(
            (k, v)[i].at[at, cols(c)], (kb, vb)[i].at[c, at], tail_sem.at[i, c])

    def head_copy(i, c):
        at = pl.ds(0, keep)
        return pltpu.make_async_copy(
            (k, v)[i].at[at, cols(c)], (kb, vb)[i].at[c, at], head_sem.at[i, c])

    def q_copy(c):
        return pltpu.make_async_copy(q.at[:, cols(c)], qb.at[c], q_sem.at[c])

    def remote(src, dst, s, r):
        return pltpu.make_async_remote_copy(
            src_ref=src, dst_ref=dst, send_sem=s, recv_sem=r,
            device_id={axis: right}, device_id_type=pl.DeviceIdType.MESH)

    def product_copy(c):
        return remote(pt.at[c], halo.at[c], send_sem.at[c], recv_sem.at[c])

    def edge_copy():
        return remote(edge_send, edge, small_send.at[0], small_recv.at[0])

    def seg_copy():
        return remote(seg, seg_prev, small_send.at[1], small_recv.at[1])

    small = [
        pltpu.make_async_copy(src, dst, small_sem.at[i])
        for i, (src, dst) in enumerate(
            ((seg_hbm, seg), (taps_hbm, taps), (filters_hbm, filters), (bias_hbm, bias)))
    ]
    small[0].start()
    for i in range(3):
        raw_copy(i).start()
    small[1].start()

    @pl.loop(0, tiles)
    def _(c):
        tail_copy(0, c).start()
        tail_copy(1, c).start()

    small[2].start()
    small[3].start()

    @pl.loop(0, tiles)
    def _(c):
        head_copy(0, c).start()
        head_copy(1, c).start()
        q_copy(c).start()

    tap = lax.broadcasted_iota(jnp.int32, (block, block), 0)
    lane = lax.broadcasted_iota(jnp.int32, (block, block), 1)

    def make_masks(b, row_before, row):
        own, early = column(row, block), column(row_before, block)
        one = jnp.where(tap == 0, pltpu.roll(early, 1, 0), pltpu.roll(own, 1, 0))
        two = jnp.where(tap < 2, pltpu.roll(early, 2, 0), pltpu.roll(own, 2, 0))
        shorts[b, 0] = jnp.where(own == one, 1.0, 0.0)
        shorts[b, 1] = jnp.where(own == two, 1.0, 0.0)
        masks[b, 0] = jnp.where((own == row_before) & (lane > tap), 1.0, 0.0).astype(BF16)
        masks[b, 1] = jnp.where((own == row) & (lane <= tap), 1.0, 0.0).astype(BF16)

    small[0].wait()
    seg0, seg1 = seg[0:1].astype(F32), seg[1:2].astype(F32)
    for i in range(3):
        raw_copy(i).wait()
    edge_send[...] = jnp.concatenate(
        [raw[i].astype(F32)[6:8] for i in range(3)] + [jnp.zeros((2, width), F32)]).astype(BF16)
    pl.semaphore_wait(barrier, has_left.astype(jnp.int32) + has_right.astype(jnp.int32))

    @pl.when(has_right)
    def _():
        seg_copy().start()
        edge_copy().start()

    make_masks(1, seg0, seg1)

    def part(c, s):
        return pl.ds(pl.multiple_of(c * tile + s, LANES), LANES)

    def taps_of(i, at):
        return taps[i, :, at].astype(F32)

    small[1].wait()

    @pl.loop(0, tiles)
    def _(c):
        tail_copy(0, c).wait()
        tail_copy(1, c).wait()
        for s in range(0, tile, LANES):
            at, here = part(c, s), slice(s, s + LANES)
            one, two = shorts[1, 0], shorts[1, 1]
            feats = []
            for i, buf in ((1, kb), (2, vb)):
                before = buf[c, keep:block, here].astype(F32)[14:16]
                feats.append(feature(buf[c, block:, here], before, taps_of(i, at), one, two))
            pt[c, :, here] = (feats[0] * feats[1]).astype(BF16)
            if s == 0:
                @pl.when(has_right & (c > 0))
                def _():
                    product_copy(jnp.maximum(c - 1, 0)).start()


    @pl.when(has_right)
    def _():
        product_copy(tiles - 1).start()

    small[2].wait()
    small[3].wait()
    turn = (tap == lax.rem(block - lane, block)).astype(BF16)
    hrev[...] = lax.dot_general(
        filters[...], turn, (((0,), (0,)), ((), ())), preferred_element_type=F32)
    biasf[...] = bias[...].astype(F32)

    @pl.when(has_left)
    def _():
        seg_copy().wait_recv()
        edge_copy().wait_recv()

    @pl.when(jnp.logical_not(has_left))
    def _():
        seg_prev[...] = jnp.zeros_like(seg_prev)
        edge[...] = jnp.zeros_like(edge)

        @pl.loop(0, tiles)
        def _(c):
            halo[c] = jnp.zeros_like(halo[c])

    make_masks(0, seg_prev[1:2].astype(F32), seg0)
    glane = lane // members

    @pl.loop(0, tiles)
    def _(c):
        head_copy(0, c).wait()
        head_copy(1, c).wait()
        q_copy(c).wait()

        @pl.when(has_left)
        def _():
            product_copy(c).wait_recv()

        for s in range(0, tile, LANES):
            at, here = part(c, s), slice(s, s + LANES)
            edges = edge[:, at].astype(F32)
            one, two = shorts[0, 0], shorts[0, 1]
            fk = feature(kb[c, :block, here], edges[2:4], taps_of(1, at), one, two)
            fv = feature(vb[c, :block, here], edges[4:6], taps_of(2, at), one, two)
            mid = (fk * fv).astype(BF16)
            far, near = halo[c, :, here], pt[c, :, here]
            first = (c * tile + s) // members
            for g in range(per):
                base = jnp.broadcast_to(hrev[pl.ds(first + g, 1), :], (block, block))
                ring = pltpu.roll(base, 0, 1, stride=1, stride_axis=0).astype(BF16)
                here_rows = slice(g * block, (g + 1) * block)
                table0[here_rows, :block] = ring * masks[0, 0]
                table0[here_rows, block:] = ring * masks[0, 1]
                table1[here_rows, :block] = ring * masks[1, 0]
                table1[here_rows, block:] = ring * masks[1, 1]
            brow = biasf[pl.ds((c * tile + s) // LANES, 1), :]
            for b, (table, low, high) in enumerate(((table0, far, mid), (table1, mid, near))):
                every = jnp.dot(table[...], jnp.concatenate([low, high], 0),
                                preferred_element_type=F32)
                for g in range(per):
                    pltpu.store(picked.at[b], every[g * block : (g + 1) * block], mask=glane == g)
                longer = picked[b] + brow * high.astype(F32)
                if b == 0:
                    before = edges[0:2]
                else:
                    before = qb[c, keep:block, here].astype(F32)[14:16]
                own = slice(b * block, (b + 1) * block)
                fq = feature(qb[c, own, here], before, taps_of(0, at), shorts[b, 0], shorts[b, 1])
                out[own, at] = (fq * longer).astype(BF16)

    @pl.when(has_right)
    def _():
        seg_copy().wait_send()
        edge_copy().wait_send()

        @pl.loop(0, tiles)
        def _(c):
            product_copy(c).wait_send()


def per_device(queries, keys, values, segments, short_filters, mr_filter, mr_bias):
    rows, width = queries.shape
    block, groups = mr_filter.shape
    members = width // groups
    tile = min(TILE, width)
    tiles = width // tile
    per = LANES // members
    dma = pltpu.SemaphoreType.DMA
    chunked = lambda r: pltpu.VMEM((tiles, r, tile), BF16)
    return pl.pallas_call(
        functools.partial(kernel, "tok", members, tiles),
        in_specs=[pl.BlockSpec(memory_space=pltpu.HBM)] * 7,
        out_specs=pl.BlockSpec(memory_space=pltpu.VMEM),
        out_shape=pltpu.VMEM((rows, width), BF16),
        scratch_shapes=[
            pltpu.VMEM((rows // block, block), jnp.int32),
            pltpu.VMEM(short_filters.shape, BF16),
            pltpu.VMEM(mr_filter.shape, BF16),
            pltpu.VMEM((width // LANES, LANES), BF16),
            chunked(rows), chunked(rows), chunked(rows),
            chunked(block), chunked(block),
            pltpu.VMEM((3, 8, width), BF16),
            pltpu.VMEM((8, width), BF16),
            pltpu.VMEM((8, width), BF16),
            pltpu.VMEM((rows // block, block), jnp.int32),
            pltpu.VMEM((groups, block), F32),
            pltpu.VMEM((width // LANES, LANES), F32),
            pltpu.VMEM((per * block, 2 * block), BF16),
            pltpu.VMEM((per * block, 2 * block), BF16),
            pltpu.VMEM((2, block, LANES), F32),
            pltpu.VMEM((2, 2, block, block), BF16),
            pltpu.VMEM((2, 2, block, block), F32),
            dma((4,)), dma((3,)), dma((2, tiles)), dma((2, tiles)), dma((tiles,)),
            dma((tiles,)), dma((tiles,)), dma((2,)), dma((2,)),
        ],
        compiler_params=pltpu.CompilerParams(
            collective_id=0, has_side_effects=True, vmem_limit_bytes=28 * 2**20
        ),
    )(*(pltpu.with_memory_space_constraint(x, pltpu.HBM) for x in (
        queries, keys, values, segments.reshape(rows // block, block), short_filters,
        mr_filter, mr_bias.reshape(width // LANES, LANES))))


def solution(mesh):
    placed = (
        P(("seq", "tok"), None),
        P(("seq", "tok"), None),
        P(("seq", "tok"), None),
        P(("seq", "tok")),
        P(),
        P(),
        P(),
    )
    return jax.shard_map(
        per_device, mesh=mesh, in_specs=placed, out_specs=P(("seq", "tok"), None), check_vma=False
    )
```
